1024 devices in a mesh: outer: 64 (over y, z_hi, core), node: 16 (over z_lo, x).
Axes of the slice: x: 4, y: 8, z: 16 (z_hi: 4, z_lo: 4; z = z_hi * 4 + z_lo), core: 2. Of those that a mesh axis runs over, the one named last changes fastest.
Arguments:
- context: bfloat16 [16384, 4096], P('outer', 'node'), may hold values from -6 to 6
- grad_out: bfloat16 [16384, 4096], P('outer', 'node'), may hold values from -6 to 6
- out_weight: bfloat16 [4096, 4096], P('node', 'outer'), may hold values from -0.09375 to 0.09375
Outputs:
- context_grad: bfloat16 [16384, 4096], P('outer', 'node')
- weight_grad: float32 [4096, 4096], P('node', 'outer')
The draws below stay inside these ranges and needn't reach their ends.
All inputs are finite; a program needn't handle non-finite values.
Results may differ from the reference program's by a relative error of at most 0.001.
Values may be sent and summed in bfloat16 or wider, within the bound.
A program may use at most 32 MiB of HBM per device.

```python
import math
import jax
import jax.numpy as jnp
from jax import lax

D_IN = 4096
DM = 4096
TOKENS = 16384


def level_of(stream_key, dims, split, least, largest):
    def one(dim, blocks):
        heights = jax.random.uniform(jax.random.fold_in(jax.random.fold_in(stream_key, 6), dim), (blocks,), jnp.float32, least / len(split), largest / len(split))
        return jnp.repeat(jnp.exp(heights), dims[dim] // blocks).reshape((-1,) + (1,) * (len(dims) - dim - 1))

    gain = one(*split[0])
    for cut in split[1:]:
        gain = gain * one(*cut)
    return gain


def centred(rng, dims, scale, bound, cuts=(), kind=jnp.bfloat16):
    loudness = level_of(rng, dims, cuts, -0.22, 0.18) if cuts else 1.0
    values = jax.random.normal(rng, dims, jnp.float32) * scale * loudness
    return jnp.minimum(jnp.maximum(values, -bound), bound).astype(kind)


def setup_inputs(seed: int = 0) -> dict:
    key_list = jax.random.split(jax.random.key(seed), 4)
    return {
        "context": centred(key_list[0], (TOKENS, D_IN), 1.0, 6.0, ((0, 64), (1, 16))),
        "grad_out": centred(key_list[1], (TOKENS, DM), 1.0, 6.0, ((0, 64), (1, 16))),
        "out_weight": centred(key_list[2], (D_IN, DM), D_IN ** -0.5, 0.09375, ((0, 16), (1, 64))),
    }


def reference(context, grad_out, out_weight):
    context_grad = lax.dot_general(grad_out, out_weight, (((1,), (1,)), ((), ())), preferred_element_type=jnp.float32).astype(jnp.bfloat16)
    weight_grad = lax.dot_general(context, grad_out, (((0,), (0,)), ((), ())), preferred_element_type=jnp.float32)
    weight_grad = weight_grad * (1.0 / math.sqrt(TOKENS))
    return (context_grad, weight_grad)
```

```python
import functools
import math

import jax
import jax.numpy as jnp
from jax import lax
from jax.experimental import pallas as pl
from jax.experimental.pallas import tpu as pltpu
from jax.sharding import PartitionSpec as P

MESH = pl.DeviceIdType.MESH
F32 = jnp.float32
NY, NZ, NC, NL, NX = 8, 4, 2, 4, 4
R = 64
HOPS = ((4, 3), (3, 4))
STEP = (1, -1)


def kernel(scale, ctx_ref, grad_ref, w_ref, cg_ref, wg_ref,
           g, gp, cp, wt, part, ry, q, rz1, rz2, acc,
           s_z, r_z, s_x, r_x, s_h, r_h, s_e, r_e, s_c, r_c,
           s_wf, r_wf, s_wh, r_wh, s_wy, r_wy, s_we, r_we,
           s_ry, r_ry, s_rz, r_rz):
    outer, node = lax.axis_index("outer"), lax.axis_index("node")
    core, zh, y = outer % NC, (outer // NC) % NZ, outer // (NC * NZ)
    zl, x = node // NX, node % NX
    other = 1 - core

    def dev(y_=None, zh_=None, core_=None, zl_=None, x_=None):
        y_ = y if y_ is None else y_
        zh_ = zh if zh_ is None else zh_
        core_ = core if core_ is None else core_
        zl_ = zl if zl_ is None else zl_
        x_ = x if x_ is None else x_
        return ((y_ * NZ + zh_) * NC + core_, zl_ * NX + x_)

    xp, xm, xo = (x + 1) % NX, (x + 3) % NX, (x + 2) % NX
    zp, zm, zo = (zh + 1) % NZ, (zh + 3) % NZ, (zh + 2) % NZ
    x_to = (dev(x_=xp), dev(x_=xm))
    z_to = (dev(zh_=zp), dev(zh_=zm))
    y_to = (dev(y_=(y + 1) % NY), dev(y_=(y + 7) % NY))
    partner = dev(core_=other)
    zl_to = [dev(zl_=(zl + k) % NL) for k in range(1, NL)]

    started = []

    def send(src, dst, ssem, rsem, to):
        copy = pltpu.make_async_remote_copy(
            src_ref=src, dst_ref=dst, send_sem=ssem, recv_sem=rsem,
            device_id=to, device_id_type=MESH)
        copy.start()
        started.append(copy)

    def arrived(dst, rsem, ssem, to):
        pltpu.make_async_remote_copy(
            src_ref=dst, dst_ref=dst, send_sem=ssem, recv_sem=rsem,
            device_id=to, device_id_type=MESH).wait_recv()

    own = grad_ref[...].T
    for j in range(2):
        for c in range(NC):
            lo = (j * NC + c) * R
            g[node, c, j] = own[lo:lo + R, :]
    wt[y, zh // 2, core, zh % 2] = w_ref[...]

    barrier = pltpu.get_barrier_semaphore()
    friends = [*x_to, *z_to, *y_to, partner, *zl_to]
    for to in friends:
        pl.semaphore_signal(barrier, inc=1, device_id=to, device_id_type=MESH)
    pl.semaphore_wait(barrier, len(friends))

    half_y = y // 2
    prio = [(half_y + 2) % NL, (half_y + 3) % NL, (half_y + 1) % NL, half_y % NL]
    place = jnp.where(prio[0] == zl, 0, jnp.where(prio[1] == zl, 1, jnp.where(prio[2] == zl, 2, 3)))
    rows = [zl]
    for i in range(1, NL):
        rows.append(jnp.where(i <= place, prio[i - 1], prio[i]))

    def blk(row, col):
        return row * NX + col

    def exchange(i, k, b):
        send(g.at[b, other], gp.at[b], s_e.at[i, k], r_e.at[i, k], partner)

    wown = wt.at[y, zh // 2, core, zh % 2]
    for d in range(2):
        send(wown, wown, s_wf.at[d], r_wf.at[d], z_to[d])
    for d in range(2):
        send(g.at[node], g.at[node], s_x.at[0, d], r_x.at[0, d], x_to[d])
    for k in range(1, NL):
        send(g.at[node], g.at[node], s_z.at[k - 1], r_z.at[k - 1], zl_to[k - 1])
    send(ctx_ref, cp, s_c, r_c, partner)
    exchange(0, 0, node)

    def forward_x(i):
        cols = (xm, xp)
        for d in range(2):
            b = blk(rows[i], cols[d])
            arrived(g.at[b], r_x.at[i, d], s_x.at[i, d], x_to[d])
            send(g.at[b, d], g.at[b, d], s_h.at[i, d], r_h.at[i, d], x_to[d])
            exchange(i, 1 + d, b)

    def finish_x(i):
        b = blk(rows[i], xo)
        for d in range(2):
            arrived(g.at[b, d], r_h.at[i, d], s_h.at[i, d], x_to[d])
        exchange(i, 3, b)

    def start_x(i):
        k = (zl - rows[i] + NL) % NL - 1
        b = blk(rows[i], x)
        arrived(g.at[b], r_z.at[k], s_z.at[k], x_to[0])
        for d in range(2):
            send(g.at[b], g.at[b], s_x.at[i, d], r_x.at[i, d], x_to[d])
        exchange(i, 0, b)

    def wslot(z_):
        return wt.at[y, z_ // 2, core, z_ % 2]

    HR = R // 2

    def forward_w():
        for d in range(2):
            z_ = (zm, zp)[d]
            arrived(wslot(z_), r_wf.at[d], s_wf.at[d], z_to[d])
            piece = wslot(z_).at[pl.ds(d * HR, HR)]
            send(piece, piece, s_wh.at[d], r_wh.at[d], z_to[d])

    def finish_w():
        for d in range(2):
            piece = wslot(zo).at[pl.ds(d * HR, HR)]
            arrived(piece, r_wh.at[d], s_wh.at[d], z_to[d])

    def wy_step(s):
        for d in range(2):
            for h in range(2):
                src = (y - STEP[d] * (s - 1) + NY) % NY
                piece = wt.at[src, h, core]
                if 1 < s <= HOPS[d][h] + 1:
                    arrived(piece, r_wy.at[d, h, s - 2], s_wy.at[d, h, s - 2], y_to[d])
                if s <= HOPS[d][h]:
                    send(piece, piece, s_wy.at[d, h, s - 1], r_wy.at[d, h, s - 1], y_to[d])

    forward_x(0)
    forward_w()
    start_x(1)
    finish_x(0)
    finish_w()
    wy_step(1)
    forward_x(1)
    start_x(2)
    wy_step(2)
    finish_x(1)
    forward_x(2)
    start_x(3)
    wy_step(3)
    finish_x(2)
    forward_x(3)
    wy_step(4)
    finish_x(3)
    wy_step(5)
    send(wt.at[:, :, core], wt.at[:, :, core], s_we, r_we, partner)

    arrived(cp, r_c, s_c, partner)
    for i in range(NL):
        for k, col in enumerate((x, xm, xp, xo)):
            b = blk(rows[i], col)
            arrived(gp.at[b], r_e.at[i, k], s_e.at[i, k], partner)

    def make_part(b):
        mine = g[b, core].reshape(2 * R, -1)
        theirs = gp[b].reshape(2 * R, -1)
        part[b] = (jnp.dot(mine, ctx_ref[...], preferred_element_type=F32)
                   + jnp.dot(theirs, cp[...], preferred_element_type=F32))

    def ry_step(s):
        for d in range(2):
            for h in range(2):
                hops = HOPS[d][h]
                if 1 < s <= hops + 1:
                    slot = ry.at[d, h, s - 2]
                    arrived(slot, r_ry.at[d, h, s - 2], s_ry.at[d, h, s - 2], y_to[d])
                if s <= hops:
                    dest = (y + STEP[d] * (hops + 1 - s) + NY) % NY
                    b = dest * 2 + h
                    if s == 1:
                        src = part.at[b]
                    else:
                        slot[...] = slot[...] + part[b]
                        src = slot
                    send(src, ry.at[d, h, s - 1], s_ry.at[d, h, s - 1], r_ry.at[d, h, s - 1], y_to[d])

    def cg_step(lo, hi):
        @pl.loop(lo, hi)
        def _(b):
            lhs = g[b].reshape(4 * R, -1)
            rhs = wt[b // 2, b % 2].reshape(4 * R, -1)
            acc[...] += lax.dot_general(lhs, rhs, (((0,), (0,)), ((), ())), preferred_element_type=F32)

    for dist in (4, 3, 5, 2, 6, 1, 7, 0):
        for h in range(2):
            make_part((y + dist) % NY * 2 + h)
        if dist == 5:
            ry_step(1)
    acc[...] = jnp.zeros_like(acc)
    arrived(wt.at[:, :, other], r_we, s_we, partner)
    cg_step(0, 6)
    ry_step(2)
    cg_step(6, 12)
    ry_step(3)
    cg_step(12, 16)
    ry_step(4)
    cg_ref[...] = acc[...].astype(cg_ref.dtype)
    ry_step(5)

    for h in range(2):
        total = part[y * 2 + h] + ry[0, h, HOPS[0][h] - 1] + ry[1, h, HOPS[1][h] - 1]
        q[2 * h] = total[:R]
        q[2 * h + 1] = total[R:]
    for d in range(2):
        send(q.at[zo, pl.ds(d * HR, HR)], rz1.at[d], s_rz.at[0, d], r_rz.at[0, d], z_to[d])
    for d in range(2):
        near = (zp, zm)[d]
        arrived(rz1.at[d], r_rz.at[0, d], s_rz.at[0, d], z_to[d])
        q[near, d * HR:(d + 1) * HR] = q[near, d * HR:(d + 1) * HR] + rz1[d]
        send(q.at[near], rz2.at[d], s_rz.at[1, d], r_rz.at[1, d], z_to[d])
    for d in range(2):
        arrived(rz2.at[d], r_rz.at[1, d], s_rz.at[1, d], z_to[d])
    wg_ref[...] = (q[zh] + rz2[0] + rz2[1]) * scale

    for copy in started:
        copy.wait_send()


def body(context, grad_out, out_weight):
    tokens, din = context.shape
    scale = 1.0 / math.sqrt(tokens * lax.axis_size("outer"))
    dma = pltpu.SemaphoreType.DMA
    bf16 = jnp.bfloat16
    vmem = pl.BlockSpec(memory_space=pltpu.VMEM)
    pairs = [(3,), (NL, 2), (NL, 2), (NL, 4), (), (2,), (2,), (2, 2, 4), (), (2, 2, 4), (2, 2)]
    sems = []
    for shape in pairs:
        sems += [dma(shape), dma(shape)]
    cg, wg = pl.pallas_call(
        functools.partial(kernel, scale),
        out_shape=(jax.ShapeDtypeStruct((tokens, din), bf16), jax.ShapeDtypeStruct((R, din), F32)),
        in_specs=[vmem] * 3,
        out_specs=(vmem, vmem),
        scratch_shapes=[
            pltpu.VMEM((NL * NX, NC, 2, R, tokens), bf16),
            pltpu.VMEM((NL * NX, 2, R, tokens), bf16),
            pltpu.VMEM((tokens, din), bf16),
            pltpu.VMEM((NY, 2, NC, 2, R, din), bf16),
            pltpu.VMEM((NL * NX, 2 * R, din), F32),
            pltpu.VMEM((2, 2, 4, 2 * R, din), F32),
            pltpu.VMEM((NZ, R, din), F32),
            pltpu.VMEM((2, R // 2, din), F32),
            pltpu.VMEM((2, R, din), F32),
            pltpu.VMEM((tokens, din), F32),
            *sems,
        ],
        compiler_params=pltpu.CompilerParams(
            collective_id=0, has_side_effects=True, vmem_limit_bytes=40 << 20),
    )(context, grad_out, jnp.transpose(out_weight))
    return (cg, jnp.transpose(wg))


def solution(mesh):
    in_specs = (P("outer", "node"), P("outer", "node"), P("node", "outer"))
    out_specs = (P("outer", "node"), P("node", "outer"))
    return jax.shard_map(body, mesh=mesh, in_specs=in_specs, out_specs=out_specs, check_vma=False)
```

```python
import functools
import math

import jax
import jax.numpy as jnp
from jax import lax
from jax.experimental import pallas as pl
from jax.experimental.pallas import tpu as pltpu
from jax.sharding import PartitionSpec as P

MESH = pl.DeviceIdType.MESH
F32 = jnp.float32
NY, NZ, NC, NL, NX = 8, 4, 2, 4, 4
R = 64
HR = R // 2
STEP = (1, -1)
HOPS = ((4, 3), (3, 4))
WHOPS = ((4, 3), (3, 4), (3, 4), (4, 3))
FL = frozenset("w g ry rz mm cg bar".split())
PLAN = (
    ("w", 0, 1), ("w", 0, 2), ("r", 1, 0, 1), ("r", 2, 0, 1), ("r", 1, 0, 0), ("r", 1, 1, 1), ("r", 2, 0, 0),
    ("r", 1, 1, 0), ("f", 0, 0, 0), ("r", 2, 1, 0), ("f", 0, 1, 0), ("wf",), ("r", 3, 0, 0), ("w", 1, 1),
    ("cp",), ("r", 3, 1, 0), ("f", 1, 0, 1), ("r", 2, 1, 1), ("n", 0, 0, 0), ("w", 2, 1), ("f", 1, 0, 0),
    ("w", 0, 3), ("o", 0, 0), ("f", 0, 0, 1), ("r", 3, 0, 1), ("n", 0, 1, 0), ("w", 1, 2), ("f", 2, 1, 0),
    ("wF",), ("f", 0, 1, 1), ("f", 1, 1, 0), ("n", 1, 0, 0), ("n", 1, 0, 1), ("f", 2, 0, 1), ("f", 2, 0, 0),
    ("n", 0, 1, 1), ("w", 3, 1), ("n", 1, 1, 0), ("w", 2, 2), ("f", 1, 1, 1), ("f", 3, 0, 0), ("f", 2, 1, 1),
    ("n", 2, 1, 0), ("n", 2, 0, 0), ("p", 1, 0, 0), ("p", 1, 1, 0), ("n", 1, 1, 1), ("w", 0, 4),
    ("p", 0, 0, 0), ("f", 3, 0, 1), ("w", 1, 3), ("f", 3, 1, 0), ("n", 3, 0, 0), ("r", 3, 1, 1), ("o", 2, 0),
    ("p", 0, 0, 1), ("n", 3, 1, 0), ("o", 1, 0), ("w", 3, 2), ("w", 2, 3), ("p", 2, 0, 0), ("o", 3, 0),
    ("n", 2, 1, 1), ("p", 3, 0, 0), ("p", 2, 0, 1), ("p", 1, 0, 1), ("p", 3, 0, 1), ("y", 0, 0, 1),
    ("f", 3, 1, 1), ("n", 3, 1, 1), ("y", 0, 0, 0), ("w", 3, 3), ("w", 2, 4), ("w", 1, 4), ("n", 2, 0, 1),
    ("o", 1, 1), ("y", 0, 1, 1), ("n", 3, 0, 1), ("o", 0, 1), ("p", 2, 1, 0), ("n", 0, 0, 1), ("o", 2, 1),
    ("p", 0, 1, 1), ("y", 0, 1, 0), ("o", 3, 1), ("p", 2, 1, 1), ("p", 3, 1, 0), ("w", 0, 5), ("p", 1, 1, 1),
    ("p", 0, 1, 0), ("p", 3, 1, 1), ("y", 1, 0, 0), ("y", 1, 0, 1), ("y", 0, 2, 1), ("w", 2, 5),
    ("y", 0, 2, 0), ("y", 1, 1, 1), ("wo", 2), ("y", 1, 1, 0), ("y", 0, 3, 0), ("y", 0, 3, 1), ("wo", 0),
    ("y", 1, 2, 1), ("wi", 2), ("y", 1, 2, 0), ("wi", 0), ("q", 0), ("c", 0), ("w", 3, 4), ("w", 1, 5),
    ("y", 1, 3, 1), ("wo", 1), ("y", 1, 3, 0), ("c", 2), ("q", 1), ("w", 3, 5), ("wi", 1), ("wo", 3),
    ("wi", 3), ("c", 3), ("c", 1), ("co",), ("ws",),
)


def kernel(scale, ctx_hbm, grad_hbm, w_hbm, cg_ref, wg_ref,
           ctx, own, g, gp, cp, wt, part, ry, q, rz, acc, ld,
           s_z, r_z, s_zf, s_x, r_x, s_h, r_h, s_e, r_e, s_c, r_c,
           s_wf, r_wf, s_wh, r_wh, s_wy, r_wy, s_we, r_we,
           s_ry, r_ry, s_rz, r_rz):
    outer, node = lax.axis_index("outer"), lax.axis_index("node")
    core, zh, y = outer % NC, (outer // NC) % NZ, outer // (NC * NZ)
    zl, x = node // NX, node % NX
    other = 1 - core

    def dev(y_=None, zh_=None, core_=None, zl_=None, x_=None):
        y_ = y if y_ is None else y_
        zh_ = zh if zh_ is None else zh_
        core_ = core if core_ is None else core_
        zl_ = zl if zl_ is None else zl_
        x_ = x if x_ is None else x_
        return ((y_ * NZ + zh_) * NC + core_, zl_ * NX + x_)

    xp, xm, xo = (x + 1) % NX, (x + 3) % NX, (x + 2) % NX
    zp, zm, zo = (zh + 1) % NZ, (zh + 3) % NZ, (zh + 2) % NZ
    x_to = (dev(x_=xp), dev(x_=xm))
    z_to = (dev(zh_=zp), dev(zh_=zm))
    y_to = (dev(y_=(y + 1) % NY), dev(y_=(y + 7) % NY))
    partner = dev(core_=other)

    loads = [
        pltpu.make_async_copy(grad_hbm, own, ld.at[0]),
        pltpu.make_async_copy(w_hbm, wt.at[y, zh // 2, core, zh % 2], ld.at[1]),
        pltpu.make_async_copy(ctx_hbm, ctx, ld.at[2]),
    ]
    for load in loads:
        load.start()
    if "bar" in FL:
        barrier = pltpu.get_barrier_semaphore()
        friends = [*x_to, *z_to, dev(zh_=zo), *y_to, partner, *(dev(zl_=(zl + k) % NL) for k in range(1, NL))]
        for to in friends:
            pl.semaphore_signal(barrier, inc=1, device_id=to, device_id_type=MESH)
    loads[0].wait()
    turned = own[...].T
    for j in range(2):
        for c in range(NC):
            lo = (j * NC + c) * R
            g[node, c, j] = turned[lo:lo + R, :]
    loads[1].wait()
    loads[2].wait()
    if "bar" in FL:
        pl.semaphore_wait(barrier, len(friends))

    started = []

    def remote(src, dst, ssem, rsem, to):
        return pltpu.make_async_remote_copy(
            src_ref=src, dst_ref=dst, send_sem=ssem, recv_sem=rsem,
            device_id=to, device_id_type=MESH)

    def send(src, dst, ssem, rsem, to, when=None):
        copy = remote(src, dst, ssem, rsem, to)
        started.append((copy, when))
        if when is None:
            copy.start()
        else:
            pl.when(when)(copy.start)

    def arrived(dst, rsem, ssem, to):
        remote(dst, dst, ssem, rsem, to).wait_recv()

    def relay(when, come, *gone):
        copies = [remote(*args) for args in gone]

        @pl.when(when)
        def _():
            remote(*come).wait_recv()
            for copy in copies:
                copy.start()
        for copy in copies:
            started.append((copy, when))

    def exchanged(i, k, b):
        return (g.at[b, other], gp.at[b], s_e.at[i, k], r_e.at[i, k], partner)

    low = zl < 2
    rows = [
        zl,
        jnp.where(low, zl + 1, zl - 1),
        jnp.where(zl == 0, 2, jnp.where(zl == 1, 0, jnp.where(zl == 2, 3, 1))),
        jnp.where(low, 3, 0),
    ]
    inner = jnp.logical_and(zl > 0, zl < NL - 1)

    par = x % 2

    def blk(row, col):
        return row * NX + col

    def exchange(i, k, b):
        send(g.at[b, other], gp.at[b], s_e.at[i, k], r_e.at[i, k], partner)

    def begin_x(i):
        b = blk(rows[i], x)
        for t in range(2):
            for d in range(2):
                c = (d, 1 - d)[t]
                send(g.at[b, c], g.at[b, c], s_x.at[i, d, c], r_x.at[i, d, c], x_to[d])

    def begin():
        wown = wt.at[y, zh // 2, core, zh % 2]
        if "w" in FL:
            for d in range(2):
                send(wown, wown, s_wf.at[d], r_wf.at[d], z_to[d])
        if "g" in FL:
            begin_x(0)
            for c in range(NC):
                piece = g.at[node, c]
                send(piece, piece, s_z.at[0, c], r_z.at[zl, c], dev(zl_=jnp.minimum(zl + 1, NL - 1)), zl < NL - 1)
                send(piece, piece, s_z.at[1, c], r_z.at[zl, c], dev(zl_=jnp.maximum(zl - 1, 0)), zl > 0)
            send(ctx, cp, s_c, r_c, partner)
            exchange(0, 0, node)

    def row_in(i, c, cl):
        if "g" not in FL:
            return
        b = blk(rows[i], x)
        onward = dev(zl_=jnp.where(inner, jnp.where(rows[i] < zl, zl + 1, zl - 1), (zl + 1) % NL))
        piece = g.at[b, c]
        mine = par == cl
        out = [(piece, piece, s_x.at[i, d, c], r_x.at[i, d, c], x_to[d]) for d in range(2)]
        if c == 1:
            out.append(exchanged(i, 0, b))
        relay(mine, (piece, piece, s_z.at[0, c], r_z.at[rows[i], c], x_to[0]), *out)
        send(piece, piece, s_zf.at[i - 1, c], r_z.at[rows[i], c], onward, jnp.logical_and(inner, mine))

    def forward_x(i, d, cl):
        if "g" not in FL:
            return
        piece = g.at[blk(rows[i], (xm, xp)[d]), d]
        relay(par != cl, (piece, piece, s_x.at[i, d, d], r_x.at[i, d, d], x_to[d]),
              (piece, piece, s_h.at[i, d], r_h.at[i, d], x_to[d]))

    def near_x(i, d, cl):
        if "g" not in FL:
            return
        b = blk(rows[i], (xm, xp)[d])
        piece = g.at[b, 1 - d]
        relay(par != cl, (piece, piece, s_x.at[i, d, 1 - d], r_x.at[i, d, 1 - d], x_to[d]), exchanged(i, 1 + d, b))

    def far_x(i, cl):
        if "g" not in FL:
            return
        b = blk(rows[i], xo)
        halves = [(g.at[b, d], g.at[b, d], s_h.at[i, d], r_h.at[i, d], x_to[d]) for d in range(2)]
        pl.when(par == cl)(lambda: remote(*halves[0]).wait_recv())
        relay(par == cl, halves[1], exchanged(i, 3, b))

    wz = (zh, zm, zp, zo)

    def wslot(z_):
        return wt.at[y, z_ // 2, core, z_ % 2]

    def forward_w():
        if "w" not in FL:
            return
        for d in range(2):
            slot = wslot(wz[1 + d])
            arrived(slot, r_wf.at[d], s_wf.at[d], z_to[d])
            piece = slot.at[pl.ds(d * HR, HR)]
            send(piece, piece, s_wh.at[d], r_wh.at[d], z_to[d])

    def finish_w():
        if "w" not in FL:
            return
        for d in range(2):
            arrived(wslot(zo).at[pl.ds(d * HR, HR)], r_wh.at[d], s_wh.at[d], z_to[d])

    def wy(k, s):
        if "w" not in FL:
            return
        for d in range(2):
            hops = WHOPS[k][d]
            piece = wt.at[(y - STEP[d] * (s - 1) + NY) % NY, wz[k] // 2, core, wz[k] % 2]
            if 1 < s <= hops + 1:
                arrived(piece, r_wy.at[k, d, s - 2], s_wy.at[k, d, s - 2], y_to[d])
            if s <= hops:
                send(piece, piece, s_wy.at[k, d, s - 1], r_wy.at[k, d, s - 1], y_to[d])

    def parts(i, cl, m):
        own_col = (x, xo)[m]
        near_col = (xm, xp)[m]
        mine = par == cl
        b = blk(rows[i], jnp.where(mine, own_col, near_col))
        if "g" in FL:
            for k, when in (((0, 3)[m], mine), ((1, 2)[m], jnp.logical_not(mine))):
                pl.when(when)(lambda k=k: arrived(gp.at[b], r_e.at[i, k], s_e.at[i, k], partner))
        if "mm" in FL:
            sums = (jnp.dot(g[b, core].reshape(2 * R, -1), ctx[...], preferred_element_type=F32)
                    + jnp.dot(gp[b].reshape(2 * R, -1), cp[...], preferred_element_type=F32))
            part[b, 0] = sums[:R]
            part[b, 1] = sums[R:]

    def hop_y(h, hop, j):
        if "ry" not in FL:
            return
        for d in range(2):
            hops = HOPS[d][j]
            if hop < hops:
                b = (y + STEP[d] * (hops - hop) + NY) % NY * 2 + h
                if hop == 0:
                    src = part.at[b, j]
                else:
                    src = ry.at[d, h, hop - 1, j]
                    arrived(src, r_ry.at[d, h, hop - 1, j], s_ry.at[d, h, hop - 1, j], y_to[d])
                    src[...] = src[...] + part[b, j]
                send(src, ry.at[d, h, hop, j], s_ry.at[d, h, hop, j], r_ry.at[d, h, hop, j], y_to[d])

    def cg_step(k):
        if "cg" not in FL:
            return
        zp_, j_ = wz[k] // 2, wz[k] % 2

        @pl.loop(0, NY)
        def _(b):
            lhs = g[b * 2 + zp_, :, j_].reshape(2 * R, -1)
            rhs = wt[b, zp_, :, j_].reshape(2 * R, -1)
            acc[...] += lax.dot_general(lhs, rhs, (((0,), (0,)), ((), ())), preferred_element_type=F32)

    def to_z(h):
        for j in range(2):
            if "ry" in FL:
                for d in range(2):
                    last = HOPS[d][j] - 1
                    arrived(ry.at[d, h, last, j], r_ry.at[d, h, last, j], s_ry.at[d, h, last, j], y_to[d])
            q[2 * h + j] = part[y * 2 + h, j] + ry[0, h, HOPS[0][j] - 1, j] + ry[1, h, HOPS[1][j] - 1, j]
        if "rz" in FL:
            for k in (2, 0, 1):
                z_ = (zp, zm, zo)[k]
                send(q.at[z_], rz.at[k], s_rz.at[k], r_rz.at[k], dev(zh_=z_), z_ // 2 == h)

    def w_block(k, c):
        return wt.at[:, wz[k] // 2, c, wz[k] % 2]

    def w_out(k):
        if "w" in FL:
            send(w_block(k, core), w_block(k, core), s_we.at[k], r_we.at[k], partner)

    def w_in(k):
        if "w" in FL:
            arrived(w_block(k, other), r_we.at[k], s_we.at[k], partner)

    def cp_in():
        if "g" in FL:
            arrived(cp, r_c, s_c, partner)

    def cg_out():
        cg_ref[...] = acc[...].astype(cg_ref.dtype)

    def settle():
        for copy, when in started:
            if when is None:
                copy.wait_send()
            else:
                pl.when(when)(copy.wait_send)
        started.clear()

    def settle_old():
        late = started[-3:]
        del started[-3:]
        settle()
        started.extend(late)

    acc[...] = jnp.zeros_like(acc)
    begin()
    steps = {
        "f": forward_x, "r": row_in, "n": near_x, "o": far_x, "p": parts, "y": hop_y, "w": wy,
        "wf": forward_w, "wF": finish_w, "wo": w_out, "wi": w_in, "cp": cp_in, "c": cg_step, "co": cg_out,
        "q": to_z, "ws": settle_old,
    }
    for name, *where in PLAN:
        steps[name](*where)

    out = q[zh]
    for k in range(3):
        if "rz" in FL:
            arrived(rz.at[k], r_rz.at[k], s_rz.at[k], partner)
        out = out + rz[k]
    wg_ref[...] = out * scale
    settle()


def body(context, grad_out, out_weight):
    tokens, din = context.shape
    scale = 1.0 / math.sqrt(tokens * lax.axis_size("outer"))
    bf16 = jnp.bfloat16
    vmem = pl.BlockSpec(memory_space=pltpu.VMEM)
    hbm = pl.BlockSpec(memory_space=pltpu.HBM)
    dma = pltpu.SemaphoreType.DMA
    sems = [dma((3,)), dma((2, 2)), dma((NL, 2)), dma((3, 2))]
    for shape in ((NL, 2, 2), (NL, 2), (NL, 4), (), (2,), (2,), (4, 2, 4), (4,), (2, 2, 4, 2), (3,)):
        sems += [dma(shape), dma(shape)]
    cg, wg = pl.pallas_call(
        functools.partial(kernel, scale),
        out_shape=(jax.ShapeDtypeStruct((tokens, din), bf16), jax.ShapeDtypeStruct((R, din), F32)),
        in_specs=[hbm] * 3,
        out_specs=(vmem, vmem),
        scratch_shapes=[
            pltpu.VMEM((tokens, din), bf16),
            pltpu.VMEM((tokens, din), bf16),
            pltpu.VMEM((NL * NX, NC, 2, R, tokens), bf16),
            pltpu.VMEM((NL * NX, 2, R, tokens), bf16),
            pltpu.VMEM((tokens, din), bf16),
            pltpu.VMEM((NY, 2, NC, 2, R, din), bf16),
            pltpu.VMEM((NL * NX, 2, R, din), F32),
            pltpu.VMEM((2, 2, 4, 2, R, din), F32),
            pltpu.VMEM((NZ, R, din), F32),
            pltpu.VMEM((3, R, din), F32),
            pltpu.VMEM((tokens, din), F32),
            *sems,
        ],
        compiler_params=pltpu.CompilerParams(
            collective_id=0, has_side_effects=True),
    )(context, grad_out, jnp.transpose(out_weight))
    return (cg, jnp.transpose(wg))


def solution(mesh):
    in_specs = (P("outer", "node"), P("outer", "node"), P("node", "outer"))
    out_specs = (P("outer", "node"), P("node", "outer"))
    return jax.shard_map(body, mesh=mesh, in_specs=in_specs, out_specs=out_specs, check_vma=False)
```

```python
import functools
import math

import jax
import jax.numpy as jnp
from jax import lax
from jax.experimental import pallas as pl
from jax.experimental.pallas import tpu as pltpu
from jax.sharding import PartitionSpec as P

MESH = pl.DeviceIdType.MESH
F32 = jnp.float32
NY, NZ, NC, NL, NX = 8, 4, 2, 4, 4
R = 64
HR = R // 2
STEP = (1, -1)
HOPS = ((4, 3), (3, 4))
WHOPS = ((4, 3), (3, 4), (3, 4), (4, 3))
PLAN = (
    ("wz",), ("w", 0, 1), ("w", 0, 2), ("r", 1, 0, 1), ("r", 2, 0, 1), ("r", 1, 0, 0), ("r", 1, 1, 1),
    ("r", 2, 0, 0), ("r", 1, 1, 0), ("f", 0, 0, 0), ("r", 2, 1, 0), ("f", 0, 1, 0), ("wf",), ("r", 3, 0, 0),
    ("w", 1, 1), ("cp",), ("r", 3, 1, 0), ("f", 1, 0, 1), ("r", 2, 1, 1), ("n", 0, 0, 0), ("w", 2, 1),
    ("f", 1, 0, 0), ("w", 0, 3), ("o", 0, 0), ("f", 0, 0, 1), ("r", 3, 0, 1), ("n", 0, 1, 0), ("w", 1, 2),
    ("f", 2, 1, 0), ("wF",), ("f", 0, 1, 1), ("f", 1, 1, 0), ("n", 1, 0, 0), ("n", 1, 0, 1), ("f", 2, 0, 1),
    ("f", 2, 0, 0), ("n", 0, 1, 1), ("w", 3, 1), ("n", 1, 1, 0), ("w", 2, 2), ("f", 1, 1, 1), ("f", 3, 0, 0),
    ("f", 2, 1, 1), ("n", 2, 1, 0), ("n", 2, 0, 0), ("p", 1, 0, 0), ("p", 1, 1, 0), ("n", 1, 1, 1),
    ("w", 0, 4), ("p", 0, 0, 0), ("f", 3, 0, 1), ("w", 1, 3), ("f", 3, 1, 0), ("n", 3, 0, 0), ("r", 3, 1, 1),
    ("o", 2, 0), ("p", 0, 0, 1), ("n", 3, 1, 0), ("o", 1, 0), ("w", 3, 2), ("w", 2, 3), ("p", 2, 0, 0),
    ("o", 3, 0), ("n", 2, 1, 1), ("p", 3, 0, 0), ("p", 2, 0, 1), ("p", 1, 0, 1), ("p", 3, 0, 1),
    ("y", 0, 0, 1), ("f", 3, 1, 1), ("n", 3, 1, 1), ("y", 0, 0, 0), ("w", 3, 3), ("w", 2, 4), ("w", 1, 4),
    ("n", 2, 0, 1), ("o", 1, 1), ("y", 0, 1, 1), ("n", 3, 0, 1), ("o", 0, 1), ("p", 2, 1, 0), ("n", 0, 0, 1),
    ("o", 2, 1), ("p", 0, 1, 1), ("y", 0, 1, 0), ("o", 3, 1), ("p", 2, 1, 1), ("p", 3, 1, 0), ("w", 0, 5),
    ("p", 1, 1, 1), ("p", 0, 1, 0), ("p", 3, 1, 1), ("y", 1, 0, 0), ("y", 1, 0, 1), ("y", 0, 2, 1),
    ("w", 2, 5), ("y", 0, 2, 0), ("y", 1, 1, 1), ("wo", 2), ("y", 1, 1, 0), ("y", 0, 3, 0), ("y", 0, 3, 1),
    ("wo", 0), ("y", 1, 2, 1), ("wi", 2), ("y", 1, 2, 0), ("wi", 0), ("q", 0), ("c", 0), ("w", 3, 4),
    ("w", 1, 5), ("y", 1, 3, 1), ("wo", 1), ("y", 1, 3, 0), ("c", 2), ("q", 1), ("w", 3, 5), ("wi", 1),
    ("wo", 3), ("wi", 3), ("c", 3), ("c", 1), ("co",), ("ws",),
)


def kernel(scale, ctx_hbm, grad_hbm, w_hbm, cg_hbm, wg_ref,
           ctx, own, g, gp, cp, wt, part, ry, q, rz, acc, ld,
           s_z, r_z, s_zf, s_x, r_x, s_h, r_h, s_e, r_e, s_c, r_c,
           s_wf, r_wf, s_wh, r_wh, s_wy, r_wy, s_we, r_we,
           s_ry, r_ry, s_rz, r_rz):
    outer, node = lax.axis_index("outer"), lax.axis_index("node")
    core, zh, y = outer % NC, (outer // NC) % NZ, outer // (NC * NZ)
    zl, x = node // NX, node % NX
    other = 1 - core

    def dev(y_=None, zh_=None, core_=None, zl_=None, x_=None):
        y_ = y if y_ is None else y_
        zh_ = zh if zh_ is None else zh_
        core_ = core if core_ is None else core_
        zl_ = zl if zl_ is None else zl_
        x_ = x if x_ is None else x_
        return ((y_ * NZ + zh_) * NC + core_, zl_ * NX + x_)

    xp, xm, xo = (x + 1) % NX, (x + 3) % NX, (x + 2) % NX
    zp, zm, zo = (zh + 1) % NZ, (zh + 3) % NZ, (zh + 2) % NZ
    x_to = (dev(x_=xp), dev(x_=xm))
    z_to = (dev(zh_=zp), dev(zh_=zm))
    y_to = (dev(y_=(y + 1) % NY), dev(y_=(y + 7) % NY))
    partner = dev(core_=other)

    loads = [
        pltpu.make_async_copy(grad_hbm, own, ld.at[0]),
        pltpu.make_async_copy(w_hbm, wt.at[y, zh // 2, core, zh % 2], ld.at[1]),
        pltpu.make_async_copy(ctx_hbm, ctx, ld.at[2]),
    ]
    for load in loads:
        load.start()
    barrier = pltpu.get_barrier_semaphore()
    friends = [*x_to, *z_to, dev(zh_=zo), *y_to, partner, *(dev(zl_=(zl + k) % NL) for k in range(1, NL))]
    for to in friends:
        pl.semaphore_signal(barrier, inc=1, device_id=to, device_id_type=MESH)
    loads[0].wait()
    turned = own[...].T
    for j in range(2):
        for c in range(NC):
            lo = (j * NC + c) * R
            g[node, c, j] = turned[lo:lo + R, :]
    loads[1].wait()
    loads[2].wait()
    pl.semaphore_wait(barrier, len(friends))

    started, final = [], []

    def remote(src, dst, ssem, rsem, to):
        return pltpu.make_async_remote_copy(
            src_ref=src, dst_ref=dst, send_sem=ssem, recv_sem=rsem,
            device_id=to, device_id_type=MESH)

    def send(src, dst, ssem, rsem, to, when=None):
        copy = remote(src, dst, ssem, rsem, to)
        started.append((copy, when))
        if when is None:
            copy.start()
        else:
            pl.when(when)(copy.start)

    def arrived(dst, rsem, ssem, to):
        remote(dst, dst, ssem, rsem, to).wait_recv()

    def relay(when, come, *gone):
        copies = [remote(*args) for args in gone]

        @pl.when(when)
        def _():
            remote(*come).wait_recv()
            for copy in copies:
                copy.start()
        for copy in copies:
            started.append((copy, when))

    def exchanged(i, k, b):
        return (g.at[b, other], gp.at[b], s_e.at[i, k], r_e.at[i, k], partner)

    low = zl < 2
    rows = [
        zl,
        jnp.where(low, zl + 1, zl - 1),
        jnp.where(zl == 0, 2, jnp.where(zl == 1, 0, jnp.where(zl == 2, 3, 1))),
        jnp.where(low, 3, 0),
    ]
    inner = jnp.logical_and(zl > 0, zl < NL - 1)

    par = x % 2

    def blk(row, col):
        return row * NX + col

    def exchange(i, k, b):
        send(g.at[b, other], gp.at[b], s_e.at[i, k], r_e.at[i, k], partner)

    def begin_x(i):
        b = blk(rows[i], x)
        for t in range(2):
            for d in range(2):
                c = (d, 1 - d)[t]
                send(g.at[b, c], g.at[b, c], s_x.at[i, d, c], r_x.at[i, d, c], x_to[d])

    def begin():
        begin_x(0)
        for c in range(NC):
            piece = g.at[node, c]
            send(piece, piece, s_z.at[0, c], r_z.at[zl, c], dev(zl_=jnp.minimum(zl + 1, NL - 1)), zl < NL - 1)
            send(piece, piece, s_z.at[1, c], r_z.at[zl, c], dev(zl_=jnp.maximum(zl - 1, 0)), zl > 0)
        send(ctx, cp, s_c, r_c, partner)
        exchange(0, 0, node)

    def row_in(i, c, cl):
        b = blk(rows[i], x)
        onward = dev(zl_=jnp.where(inner, jnp.where(rows[i] < zl, zl + 1, zl - 1), (zl + 1) % NL))
        piece = g.at[b, c]
        mine = par == cl
        out = [(piece, piece, s_x.at[i, d, c], r_x.at[i, d, c], x_to[d]) for d in range(2)]
        if c == 1:
            out.append(exchanged(i, 0, b))
        relay(mine, (piece, piece, s_z.at[0, c], r_z.at[rows[i], c], x_to[0]), *out)
        send(piece, piece, s_zf.at[i - 1, c], r_z.at[rows[i], c], onward, jnp.logical_and(inner, mine))

    def forward_x(i, d, cl):
        piece = g.at[blk(rows[i], (xm, xp)[d]), d]
        relay(par != cl, (piece, piece, s_x.at[i, d, d], r_x.at[i, d, d], x_to[d]),
              (piece, piece, s_h.at[i, d], r_h.at[i, d], x_to[d]))

    def near_x(i, d, cl):
        b = blk(rows[i], (xm, xp)[d])
        piece = g.at[b, 1 - d]
        relay(par != cl, (piece, piece, s_x.at[i, d, 1 - d], r_x.at[i, d, 1 - d], x_to[d]), exchanged(i, 1 + d, b))

    def far_x(i, cl):
        b = blk(rows[i], xo)
        halves = [(g.at[b, d], g.at[b, d], s_h.at[i, d], r_h.at[i, d], x_to[d]) for d in range(2)]
        pl.when(par == cl)(lambda: remote(*halves[0]).wait_recv())
        relay(par == cl, halves[1], exchanged(i, 3, b))

    wz = (zh, zm, zp, zo)

    def wslot(z_):
        return wt.at[y, z_ // 2, core, z_ % 2]

    def begin_w():
        for d in range(2):
            send(wslot(zh), wslot(zh), s_wf.at[d], r_wf.at[d], z_to[d])

    def forward_w():
        for d in range(2):
            slot = wslot(wz[1 + d])
            arrived(slot, r_wf.at[d], s_wf.at[d], z_to[d])
            piece = slot.at[pl.ds(d * HR, HR)]
            send(piece, piece, s_wh.at[d], r_wh.at[d], z_to[d])

    def finish_w():
        for d in range(2):
            arrived(wslot(zo).at[pl.ds(d * HR, HR)], r_wh.at[d], s_wh.at[d], z_to[d])

    def wy(k, s):
        for d in range(2):
            hops = WHOPS[k][d]
            piece = wt.at[(y - STEP[d] * (s - 1) + NY) % NY, wz[k] // 2, core, wz[k] % 2]
            if 1 < s <= hops + 1:
                arrived(piece, r_wy.at[k, d, s - 2], s_wy.at[k, d, s - 2], y_to[d])
            if s <= hops:
                send(piece, piece, s_wy.at[k, d, s - 1], r_wy.at[k, d, s - 1], y_to[d])

    def parts(i, cl, m):
        own_col = (x, xo)[m]
        near_col = (xm, xp)[m]
        mine = par == cl
        b = blk(rows[i], jnp.where(mine, own_col, near_col))
        for k, when in (((0, 3)[m], mine), ((1, 2)[m], jnp.logical_not(mine))):
            pl.when(when)(lambda k=k: arrived(gp.at[b], r_e.at[i, k], s_e.at[i, k], partner))
        sums = (jnp.dot(g[b, core].reshape(2 * R, -1), ctx[...], preferred_element_type=F32)
                + jnp.dot(gp[b].reshape(2 * R, -1), cp[...], preferred_element_type=F32))
        part[b, 0] = sums[:R]
        part[b, 1] = sums[R:]

    def hop_y(h, hop, j):
        for d in range(2):
            hops = HOPS[d][j]
            if hop < hops:
                b = (y + STEP[d] * (hops - hop) + NY) % NY * 2 + h
                if hop == 0:
                    src = part.at[b, j]
                else:
                    src = ry.at[d, h, hop - 1, j]
                    arrived(src, r_ry.at[d, h, hop - 1, j], s_ry.at[d, h, hop - 1, j], y_to[d])
                    src[...] = src[...] + part[b, j]
                send(src, ry.at[d, h, hop, j], s_ry.at[d, h, hop, j], r_ry.at[d, h, hop, j], y_to[d])

    def cg_step(k):
        zp_, j_ = wz[k] // 2, wz[k] % 2

        lhs = jnp.concatenate([g[b * 2 + zp_, :, j_].reshape(2 * R, -1) for b in range(NY)], axis=0)
        rhs = jnp.concatenate([wt[b, zp_, :, j_].reshape(2 * R, -1) for b in range(NY)], axis=0)
        acc[...] += lax.dot_general(lhs, rhs, (((0,), (0,)), ((), ())), preferred_element_type=F32)

    def to_z(h):
        for j in range(2):
            for d in range(2):
                last = HOPS[d][j] - 1
                arrived(ry.at[d, h, last, j], r_ry.at[d, h, last, j], s_ry.at[d, h, last, j], y_to[d])
            q[2 * h + j] = part[y * 2 + h, j] + ry[0, h, HOPS[0][j] - 1, j] + ry[1, h, HOPS[1][j] - 1, j]
        for k in (2, 0, 1):
            z_ = (zp, zm, zo)[k]
            copy = remote(q.at[z_], rz.at[k], s_rz.at[k], r_rz.at[k], dev(zh_=z_))
            pl.when(z_ // 2 == h)(copy.start)
            if h:
                final.append((copy, None))

    def w_block(k, c):
        return wt.at[:, wz[k] // 2, c, wz[k] % 2]

    def w_out(k):
        send(w_block(k, core), w_block(k, core), s_we.at[k], r_we.at[k], partner)

    def w_in(k):
        arrived(w_block(k, other), r_we.at[k], s_we.at[k], partner)

    def cp_in():
        arrived(cp, r_c, s_c, partner)

    cg_copy = pltpu.make_async_copy(own, cg_hbm, ld.at[0])

    def cg_out():
        own[...] = acc[...].astype(own.dtype)
        cg_copy.start()

    def settle(copies):
        for copy, when in copies:
            if when is None:
                copy.wait_send()
            else:
                pl.when(when)(copy.wait_send)

    acc[...] = jnp.zeros_like(acc)
    begin()
    steps = {
        "f": forward_x, "r": row_in, "n": near_x, "o": far_x, "p": parts, "y": hop_y, "w": wy,
        "wz": begin_w, "wf": forward_w, "wF": finish_w, "wo": w_out, "wi": w_in, "cp": cp_in, "c": cg_step, "co": cg_out,
        "q": to_z, "ws": lambda: settle(started),
    }
    for name, *where in PLAN:
        steps[name](*where)

    out = q[zh]
    for k in range(3):
        arrived(rz.at[k], r_rz.at[k], s_rz.at[k], partner)
        out = out + rz[k]
    wg_ref[...] = out * scale
    settle(final)
    cg_copy.wait()


def body(context, grad_out, out_weight):
    tokens, din = context.shape
    scale = 1.0 / math.sqrt(tokens * lax.axis_size("outer"))
    bf16 = jnp.bfloat16
    vmem = pl.BlockSpec(memory_space=pltpu.VMEM)
    hbm = pl.BlockSpec(memory_space=pltpu.HBM)
    dma = pltpu.SemaphoreType.DMA
    sems = [dma((3,)), dma((2, 2)), dma((NL, 2)), dma((3, 2))]
    for shape in ((NL, 2, 2), (NL, 2), (NL, 4), (), (2,), (2,), (4, 2, 4), (4,), (2, 2, 4, 2), (3,)):
        sems += [dma(shape), dma(shape)]
    cg, wg = pl.pallas_call(
        functools.partial(kernel, scale),
        out_shape=(jax.ShapeDtypeStruct((tokens, din), bf16), jax.ShapeDtypeStruct((R, din), F32)),
        in_specs=[hbm] * 3,
        out_specs=(hbm, vmem),
        scratch_shapes=[
            pltpu.VMEM((tokens, din), bf16),
            pltpu.VMEM((tokens, din), bf16),
            pltpu.VMEM((NL * NX, NC, 2, R, tokens), bf16),
            pltpu.VMEM((NL * NX, 2, R, tokens), bf16),
            pltpu.VMEM((tokens, din), bf16),
            pltpu.VMEM((NY, 2, NC, 2, R, din), bf16),
            pltpu.VMEM((NL * NX, 2, R, din), F32),
            pltpu.VMEM((2, 2, 4, 2, R, din), F32),
            pltpu.VMEM((NZ, R, din), F32),
            pltpu.VMEM((3, R, din), F32),
            pltpu.VMEM((tokens, din), F32),
            *sems,
        ],
        compiler_params=pltpu.CompilerParams(
            collective_id=0, has_side_effects=True),
    )(context, grad_out, jnp.transpose(out_weight))
    return (cg, jnp.transpose(wg))


def solution(mesh):
    in_specs = (P("outer", "node"), P("outer", "node"), P("node", "outer"))
    out_specs = (P("outer", "node"), P("node", "outer"))
    return jax.shard_map(body, mesh=mesh, in_specs=in_specs, out_specs=out_specs, check_vma=False)
```

```python
import functools
import math

import jax
import jax.numpy as jnp
from jax import lax
from jax.experimental import pallas as pl
from jax.experimental.pallas import tpu as pltpu
from jax.sharding import PartitionSpec as P

MESH = pl.DeviceIdType.MESH
F32 = jnp.float32
NY, NZ, NC, NL, NX = 8, 4, 2, 4, 4
R = 64
HR = R // 2
STEP = (1, -1)
HOPS = ((4, 3), (3, 4))
WHOPS = ((4, 3), (3, 4), (3, 4), (4, 3))
PLAN = (
    ("wz",), ("w", 0, 1), ("w", 0, 2), ("r", 1, 0, 1), ("r", 2, 0, 1), ("r", 1, 0, 0), ("r", 1, 1, 1),
    ("r", 2, 0, 0), ("r", 1, 1, 0), ("f", 0, 0, 0), ("r", 2, 1, 0), ("f", 0, 1, 0), ("wf",), ("r", 3, 0, 0),
    ("w", 1, 1), ("cp",), ("r", 3, 1, 0), ("f", 1, 0, 1), ("r", 2, 1, 1), ("n", 0, 0, 0), ("w", 2, 1),
    ("f", 1, 0, 0), ("w", 0, 3), ("o", 0, 0), ("f", 0, 0, 1), ("r", 3, 0, 1), ("n", 0, 1, 0), ("w", 1, 2),
    ("f", 2, 1, 0), ("wF",), ("f", 0, 1, 1), ("f", 1, 1, 0), ("n", 1, 0, 0), ("n", 1, 0, 1), ("f", 2, 0, 1),
    ("f", 2, 0, 0), ("n", 0, 1, 1), ("w", 3, 1), ("n", 1, 1, 0), ("w", 2, 2), ("f", 1, 1, 1), ("f", 3, 0, 0),
    ("f", 2, 1, 1), ("n", 2, 1, 0), ("n", 2, 0, 0), ("p", 1, 0, 0), ("p", 1, 1, 0), ("n", 1, 1, 1),
    ("w", 0, 4), ("p", 0, 0, 0), ("f", 3, 0, 1), ("w", 1, 3), ("f", 3, 1, 0), ("n", 3, 0, 0), ("r", 3, 1, 1),
    ("o", 2, 0), ("p", 0, 0, 1), ("n", 3, 1, 0), ("o", 1, 0), ("w", 3, 2), ("w", 2, 3), ("p", 2, 0, 0),
    ("o", 3, 0), ("n", 2, 1, 1), ("p", 3, 0, 0), ("p", 2, 0, 1), ("p", 1, 0, 1), ("p", 3, 0, 1),
    ("y", 0, 0, 1), ("f", 3, 1, 1), ("n", 3, 1, 1), ("y", 0, 0, 0), ("w", 3, 3), ("w", 2, 4), ("w", 1, 4),
    ("n", 2, 0, 1), ("o", 1, 1), ("y", 0, 1, 1), ("n", 3, 0, 1), ("o", 0, 1), ("p", 2, 1, 0), ("n", 0, 0, 1),
    ("o", 2, 1), ("p", 0, 1, 1), ("y", 0, 1, 0), ("o", 3, 1), ("p", 2, 1, 1), ("p", 3, 1, 0), ("w", 0, 5),
    ("p", 1, 1, 1), ("p", 0, 1, 0), ("p", 3, 1, 1), ("y", 1, 0, 0), ("y", 1, 0, 1), ("y", 0, 2, 1),
    ("w", 2, 5), ("y", 0, 2, 0), ("y", 1, 1, 1), ("wo", 2), ("y", 1, 1, 0), ("y", 0, 3, 0), ("y", 0, 3, 1),
    ("wo", 0), ("y", 1, 2, 1), ("wi", 2), ("y", 1, 2, 0), ("wi", 0), ("q", 0), ("c", 0), ("w", 3, 4),
    ("w", 1, 5), ("y", 1, 3, 1), ("wo", 1), ("y", 1, 3, 0), ("c", 2), ("q", 1), ("w", 3, 5), ("wi", 1),
    ("wo", 3), ("wi", 3), ("c", 3), ("c", 1), ("co",), ("ws",),
)


def kernel(scale, ctx_hbm, grad_hbm, w_hbm, cg_hbm, wg_ref,
           ctx, own, g, gp, cp, wt, part, ry, q, rz, acc, ld,
           s_z, r_z, s_zf, s_x, r_x, s_h, r_h, s_e, r_e, s_c, r_c,
           s_wf, r_wf, s_wh, r_wh, s_wy, r_wy, s_we, r_we,
           s_ry, r_ry, s_rz, r_rz):
    outer, node = lax.axis_index("outer"), lax.axis_index("node")
    core, zh, y = outer % NC, (outer // NC) % NZ, outer // (NC * NZ)
    zl, x = node // NX, node % NX
    other = 1 - core

    def dev(y_=None, zh_=None, core_=None, zl_=None, x_=None):
        y_ = y if y_ is None else y_
        zh_ = zh if zh_ is None else zh_
        core_ = core if core_ is None else core_
        zl_ = zl if zl_ is None else zl_
        x_ = x if x_ is None else x_
        return ((y_ * NZ + zh_) * NC + core_, zl_ * NX + x_)

    xp, xm, xo = (x + 1) % NX, (x + 3) % NX, (x + 2) % NX
    zp, zm, zo = (zh + 1) % NZ, (zh + 3) % NZ, (zh + 2) % NZ
    x_to = (dev(x_=xp), dev(x_=xm))
    z_to = (dev(zh_=zp), dev(zh_=zm))
    y_to = (dev(y_=(y + 1) % NY), dev(y_=(y + 7) % NY))
    partner = dev(core_=other)

    loads = [
        pltpu.make_async_copy(grad_hbm, own, ld.at[0]),
        pltpu.make_async_copy(w_hbm, wt.at[y, zh // 2, core, zh % 2], ld.at[1]),
        pltpu.make_async_copy(ctx_hbm, ctx, ld.at[2]),
    ]
    for load in loads:
        load.start()
    barrier = pltpu.get_barrier_semaphore()
    friends = [*x_to, *z_to, dev(zh_=zo), *y_to, partner, *(dev(zl_=(zl + k) % NL) for k in range(1, NL))]
    for to in friends:
        pl.semaphore_signal(barrier, inc=1, device_id=to, device_id_type=MESH)
    loads[0].wait()
    turned = own[...].T
    for j in range(2):
        for c in range(NC):
            lo = (j * NC + c) * R
            g[node, c, j] = turned[lo:lo + R, :]
    loads[1].wait()
    loads[2].wait()
    acc[...] = jnp.zeros_like(acc)
    pl.semaphore_wait(barrier, len(friends))

    started, final = [], []

    def remote(src, dst, ssem, rsem, to):
        return pltpu.make_async_remote_copy(
            src_ref=src, dst_ref=dst, send_sem=ssem, recv_sem=rsem,
            device_id=to, device_id_type=MESH)

    def send(src, dst, ssem, rsem, to, when=None):
        copy = remote(src, dst, ssem, rsem, to)
        started.append((copy, when))
        if when is None:
            copy.start()
        else:
            pl.when(when)(copy.start)

    def arrived(dst, rsem, ssem, to):
        remote(dst, dst, ssem, rsem, to).wait_recv()

    def relay(when, come, *gone):
        copies = [remote(*args) for args in gone]

        @pl.when(when)
        def _():
            remote(*come).wait_recv()
            for copy in copies:
                copy.start()
        for copy in copies:
            started.append((copy, when))

    def exchanged(i, k, b):
        return (g.at[b, other], gp.at[b], s_e.at[i, k], r_e.at[i, k], partner)

    low = zl < 2
    rows = [
        zl,
        jnp.where(low, zl + 1, zl - 1),
        jnp.where(zl == 0, 2, jnp.where(zl == 1, 0, jnp.where(zl == 2, 3, 1))),
        jnp.where(low, 3, 0),
    ]
    inner = jnp.logical_and(zl > 0, zl < NL - 1)

    par = x % 2

    def blk(row, col):
        return row * NX + col

    def exchange(i, k, b):
        send(g.at[b, other], gp.at[b], s_e.at[i, k], r_e.at[i, k], partner)

    def begin_x(i):
        b = blk(rows[i], x)
        for t in range(2):
            for d in range(2):
                c = (d, 1 - d)[t]
                send(g.at[b, c], g.at[b, c], s_x.at[i, d, c], r_x.at[i, d, c], x_to[d])

    def begin():
        begin_x(0)
        for c in range(NC):
            piece = g.at[node, c]
            send(piece, piece, s_z.at[0, c], r_z.at[zl, c], dev(zl_=jnp.minimum(zl + 1, NL - 1)), zl < NL - 1)
            send(piece, piece, s_z.at[1, c], r_z.at[zl, c], dev(zl_=jnp.maximum(zl - 1, 0)), zl > 0)
        send(ctx, cp, s_c, r_c, partner)
        exchange(0, 0, node)

    def row_in(i, c, cl):
        b = blk(rows[i], x)
        onward = dev(zl_=jnp.where(inner, jnp.where(rows[i] < zl, zl + 1, zl - 1), (zl + 1) % NL))
        piece = g.at[b, c]
        mine = par == cl
        out = [(piece, piece, s_x.at[i, d, c], r_x.at[i, d, c], x_to[d]) for d in range(2)]
        if c == 1:
            out.append(exchanged(i, 0, b))
        relay(mine, (piece, piece, s_z.at[0, c], r_z.at[rows[i], c], x_to[0]), *out)
        send(piece, piece, s_zf.at[i - 1, c], r_z.at[rows[i], c], onward, jnp.logical_and(inner, mine))

    def forward_x(i, d, cl):
        piece = g.at[blk(rows[i], (xm, xp)[d]), d]
        relay(par != cl, (piece, piece, s_x.at[i, d, d], r_x.at[i, d, d], x_to[d]),
              (piece, piece, s_h.at[i, d], r_h.at[i, d], x_to[d]))

    def near_x(i, d, cl):
        b = blk(rows[i], (xm, xp)[d])
        piece = g.at[b, 1 - d]
        relay(par != cl, (piece, piece, s_x.at[i, d, 1 - d], r_x.at[i, d, 1 - d], x_to[d]), exchanged(i, 1 + d, b))

    def far_x(i, cl):
        b = blk(rows[i], xo)
        halves = [(g.at[b, d], g.at[b, d], s_h.at[i, d], r_h.at[i, d], x_to[d]) for d in range(2)]
        pl.when(par == cl)(lambda: remote(*halves[0]).wait_recv())
        relay(par == cl, halves[1], exchanged(i, 3, b))

    wz = (zh, zm, zp, zo)

    def wslot(z_):
        return wt.at[y, z_ // 2, core, z_ % 2]

    def begin_w():
        for d in range(2):
            send(wslot(zh), wslot(zh), s_wf.at[d], r_wf.at[d], z_to[d])

    def forward_w():
        for d in range(2):
            slot = wslot(wz[1 + d])
            arrived(slot, r_wf.at[d], s_wf.at[d], z_to[d])
            piece = slot.at[pl.ds(d * HR, HR)]
            send(piece, piece, s_wh.at[d], r_wh.at[d], z_to[d])

    def finish_w():
        for d in range(2):
            arrived(wslot(zo).at[pl.ds(d * HR, HR)], r_wh.at[d], s_wh.at[d], z_to[d])

    def wy(k, s):
        for d in range(2):
            hops = WHOPS[k][d]
            piece = wt.at[(y - STEP[d] * (s - 1) + NY) % NY, wz[k] // 2, core, wz[k] % 2]
            if 1 < s <= hops + 1:
                arrived(piece, r_wy.at[k, d, s - 2], s_wy.at[k, d, s - 2], y_to[d])
            if s <= hops:
                send(piece, piece, s_wy.at[k, d, s - 1], r_wy.at[k, d, s - 1], y_to[d])

    def parts(i, cl, m):
        own_col = (x, xo)[m]
        near_col = (xm, xp)[m]
        mine = par == cl
        b = blk(rows[i], jnp.where(mine, own_col, near_col))
        for k, when in (((0, 3)[m], mine), ((1, 2)[m], jnp.logical_not(mine))):
            pl.when(when)(lambda k=k: arrived(gp.at[b], r_e.at[i, k], s_e.at[i, k], partner))
        sums = (jnp.dot(g[b, core].reshape(2 * R, -1), ctx[...], preferred_element_type=F32)
                + jnp.dot(gp[b].reshape(2 * R, -1), cp[...], preferred_element_type=F32))
        part[b, 0] = sums[:R]
        part[b, 1] = sums[R:]

    def hop_y(h, hop, j):
        for d in range(2):
            hops = HOPS[d][j]
            if hop < hops:
                b = (y + STEP[d] * (hops - hop) + NY) % NY * 2 + h
                if hop == 0:
                    src = part.at[b, j]
                else:
                    src = ry.at[d, h, hop - 1, j]
                    arrived(src, r_ry.at[d, h, hop - 1, j], s_ry.at[d, h, hop - 1, j], y_to[d])
                    src[...] = src[...] + part[b, j]
                send(src, ry.at[d, h, hop, j], s_ry.at[d, h, hop, j], r_ry.at[d, h, hop, j], y_to[d])

    def cg_step(k):
        zp_, j_ = wz[k] // 2, wz[k] % 2

        lhs = jnp.concatenate([g[b * 2 + zp_, :, j_].reshape(2 * R, -1) for b in range(NY)], axis=0)
        rhs = jnp.concatenate([wt[b, zp_, :, j_].reshape(2 * R, -1) for b in range(NY)], axis=0)
        acc[...] += lax.dot_general(lhs, rhs, (((0,), (0,)), ((), ())), preferred_element_type=F32)

    def to_z(h):
        for j in range(2):
            for d in range(2):
                last = HOPS[d][j] - 1
                arrived(ry.at[d, h, last, j], r_ry.at[d, h, last, j], s_ry.at[d, h, last, j], y_to[d])
            q[2 * h + j] = part[y * 2 + h, j] + ry[0, h, HOPS[0][j] - 1, j] + ry[1, h, HOPS[1][j] - 1, j]
            for k in (2, 0, 1):
                z_ = (zp, zm, zo)[k]
                copy = remote(q.at[z_], rz.at[k], s_rz.at[k], r_rz.at[k], dev(zh_=z_))
                pl.when(z_ == 2 * h + j)(copy.start)
                if h + j == 2:
                    final.append((copy, None))

    def w_block(k, c):
        return wt.at[:, wz[k] // 2, c, wz[k] % 2]

    def w_out(k):
        send(w_block(k, core), w_block(k, core), s_we.at[k], r_we.at[k], partner)

    def w_in(k):
        arrived(w_block(k, other), r_we.at[k], s_we.at[k], partner)

    def cp_in():
        arrived(cp, r_c, s_c, partner)

    cg_copy = pltpu.make_async_copy(own, cg_hbm, ld.at[0])

    def cg_out():
        own[...] = acc[...].astype(own.dtype)
        cg_copy.start()

    def settle(copies):
        for copy, when in copies:
            if when is None:
                copy.wait_send()
            else:
                pl.when(when)(copy.wait_send)

    begin()
    steps = {
        "f": forward_x, "r": row_in, "n": near_x, "o": far_x, "p": parts, "y": hop_y, "w": wy,
        "wz": begin_w, "wf": forward_w, "wF": finish_w, "wo": w_out, "wi": w_in, "cp": cp_in, "c": cg_step, "co": cg_out,
        "q": to_z, "ws": lambda: settle(started),
    }
    for name, *where in PLAN:
        steps[name](*where)

    out = q[zh]
    for k in range(3):
        arrived(rz.at[k], r_rz.at[k], s_rz.at[k], partner)
        out = out + rz[k]
    wg_ref[...] = out * scale
    settle(final)
    cg_copy.wait()


def body(context, grad_out, out_weight):
    tokens, din = context.shape
    scale = 1.0 / math.sqrt(tokens * lax.axis_size("outer"))
    bf16 = jnp.bfloat16
    vmem = pl.BlockSpec(memory_space=pltpu.VMEM)
    hbm = pl.BlockSpec(memory_space=pltpu.HBM)
    dma = pltpu.SemaphoreType.DMA
    sems = [dma((3,)), dma((2, 2)), dma((NL, 2)), dma((3, 2))]
    for shape in ((NL, 2, 2), (NL, 2), (NL, 4), (), (2,), (2,), (4, 2, 4), (4,), (2, 2, 4, 2), (3,)):
        sems += [dma(shape), dma(shape)]
    cg, wg = pl.pallas_call(
        functools.partial(kernel, scale),
        out_shape=(jax.ShapeDtypeStruct((tokens, din), bf16), jax.ShapeDtypeStruct((R, din), F32)),
        in_specs=[hbm] * 3,
        out_specs=(hbm, vmem),
        scratch_shapes=[
            pltpu.VMEM((tokens, din), bf16),
            pltpu.VMEM((tokens, din), bf16),
            pltpu.VMEM((NL * NX, NC, 2, R, tokens), bf16),
            pltpu.VMEM((NL * NX, 2, R, tokens), bf16),
            pltpu.VMEM((tokens, din), bf16),
            pltpu.VMEM((NY, 2, NC, 2, R, din), bf16),
            pltpu.VMEM((NL * NX, 2, R, din), F32),
            pltpu.VMEM((2, 2, 4, 2, R, din), F32),
            pltpu.VMEM((NZ, R, din), F32),
            pltpu.VMEM((3, R, din), F32),
            pltpu.VMEM((tokens, din), F32),
            *sems,
        ],
        compiler_params=pltpu.CompilerParams(
            collective_id=0, has_side_effects=True),
    )(context, grad_out, jnp.transpose(out_weight))
    return (cg, jnp.transpose(wg))


def solution(mesh):
    in_specs = (P("outer", "node"), P("outer", "node"), P("node", "outer"))
    out_specs = (P("outer", "node"), P("node", "outer"))
    return jax.shard_map(body, mesh=mesh, in_specs=in_specs, out_specs=out_specs, check_vma=False)
```
